32 devices in a mesh: dp: 16 (over z, y, core), tensor: 2 (over x).
Axes of the slice: x: 2, y: 2, z: 4, core: 2. Of those that a mesh axis runs over, the one named last changes fastest.
Arguments:
- tokens: bfloat16 [64, 256, 1152], P(('dp', 'tensor')), may hold values from -6 to 6
- condition: bfloat16 [64, 1152], P('dp', 'tensor'), may hold values from -6 to 6
- keep_count: int32 [64], P('dp'), may hold values from 64 to 192, as said below
- token_order: int32 [64, 256], P(('dp', 'tensor')), may hold values from 0 to 255, each once within a row
- w_ada: bfloat16 [1152, 6912], P('tensor'), may hold values from -0.1875 to 0.1875
- b_ada: bfloat16 [6912], replicated, may hold values from -3 to 3
- w_qkv: bfloat16 [1152, 3, 1152], P(None, None, 'tensor'), may hold values from -0.1875 to 0.1875
- b_qv: bfloat16 [2, 1152], P(None, 'tensor'), may hold values from -3 to 3
- w_proj: bfloat16 [1152, 1152], P('tensor'), may hold values from -0.5 to 0.5
- b_proj: bfloat16 [1152], replicated, may hold values from -2 to 2
- w_up: bfloat16 [1152, 4608], P(None, 'tensor'), may hold values from -0.1875 to 0.1875
- b_up: bfloat16 [4608], P('tensor'), may hold values from -3 to 3
- w_down: bfloat16 [4608, 1152], P('tensor'), may hold values from -0.09375 to 0.09375
- b_down: bfloat16 [1152], replicated, may hold values from -2 to 2
- cotangent: bfloat16 [64, 256, 1152], P(('dp', 'tensor')), may hold values from -6 to 6
Outputs:
- block_out: bfloat16 [64, 256, 1152], P(('dp', 'tensor'))
- grad_tokens: float32 [64, 256, 1152], P(('dp', 'tensor'))
- grad_condition: float32 [64, 1152], P('dp', 'tensor')
- grad_w_ada: float32 [1152, 6912], P('tensor')
- grad_b_ada: float32 [6912], replicated
- grad_w_qkv: float32 [1152, 3, 1152], P(None, None, 'tensor')
- grad_b_qv: float32 [2, 1152], P(None, 'tensor')
- grad_w_proj: float32 [1152, 1152], P('tensor')
- grad_b_proj: float32 [1152], replicated
- grad_w_up: float32 [1152, 4608], P(None, 'tensor')
- grad_b_up: float32 [4608], P('tensor')
- grad_w_down: float32 [4608, 1152], P('tensor')
- grad_b_down: float32 [1152], replicated
The draws below stay inside these ranges and needn't reach their ends.
Inputs may be any that keep to these rules, and one draw needn't show every extreme that they name: Image i keeps the tokens at token_order[i, 0] to token_order[i, keep_count[i] - 1]; in every draw some image keeps 192. `token_order`: each row is a permutation of 0 to 255.
All inputs are finite; a program needn't handle non-finite values.
Results may differ from the reference program's by a relative error of at most 0.022.
The reference program's roundings to bfloat16 on the way count: a program that leaves them out, or rounds other values in their place, can miss the bound.
Values may be sent and summed in bfloat16 or wider, within the bound.
No kernel may reach another device: no remote copies, remote signals or barrier semaphores. Data moves between devices by JAX's collectives and lax.ppermute only.
A program may use at most 192 MiB of HBM per device.

```python
import jax
import jax.numpy as jnp
from jax import lax

D = 1152
HEADS = 16
HD = 72
FF = 4608
SEQ = 256
IMAGES = 64


def draw_keep_count(key, part):
    key_counts, key_pick, key_index = jax.random.split(jax.random.fold_in(key, 11), 3)
    lowest_count = SEQ // 4
    highest_count = 3 * SEQ // 4
    counts = jax.random.randint(key_counts, (IMAGES,), lowest_count, highest_count + 1)
    chosen = jax.random.randint(key_pick, (IMAGES,), 0, 8)
    forced = jax.random.randint(key_index, (), 0, IMAGES)
    image_ids = jnp.arange(IMAGES, dtype=jnp.int32)
    full_image = (chosen == 0) | (image_ids == forced)
    return jnp.where(full_image, highest_count, counts).astype(jnp.int32)


def block_scale(rng, dims, cuts, least, largest):
    loudness, own = 1.0, jax.random.fold_in(rng, 6)
    for dim, blocks in cuts:
        steps = jnp.exp(jax.random.uniform(jax.random.fold_in(own, dim), (blocks,), jnp.float32, least / len(cuts), largest / len(cuts)))
        loudness = loudness * jnp.repeat(steps, dims[dim] // blocks).reshape([-1 if axis == dim else 1 for axis in range(len(dims))])
    return loudness


def scatter_about(own_key, shape, spread, limit, cuts=(), held_as=jnp.bfloat16):
    entries = spread * jax.random.normal(own_key, shape, jnp.float32)
    if cuts:
        entries = entries * block_scale(own_key, shape, cuts, -0.22, 0.18)
    return jnp.clip(entries, -limit, limit).astype(held_as)


def setup_inputs(seed: int = 0) -> dict:
    streams_of = jax.random.split(jax.random.key(seed), 16)
    return {
        "tokens": scatter_about(streams_of[0], (IMAGES, SEQ, D), 1.0, 6.0, ((0, 32),)),
        "condition": scatter_about(streams_of[1], (IMAGES, D), 1.0, 6.0, ((0, 16), (1, 2))),
        "keep_count": draw_keep_count(jax.random.fold_in(streams_of[15], 71), 0),
        "token_order": jax.vmap(lambda own: jax.random.permutation(own, SEQ))(jax.random.split(streams_of[3], IMAGES)).reshape((IMAGES, SEQ)).astype(jnp.int32),
        "w_ada": scatter_about(streams_of[4], (D, 6 * D), D ** -0.5, 0.1875, ((0, 2),)),
        "b_ada": scatter_about(streams_of[5], (6 * D,), 0.5, 3.0),
        "w_qkv": scatter_about(streams_of[6], (D, 3, D), D ** -0.5, 0.1875, ((2, 2),)),
        "b_qv": scatter_about(streams_of[7], (2, D), 0.5, 3.0, ((1, 2),)),
        "w_proj": scatter_about(streams_of[8], (D, D), (D // 8) ** -0.5, 0.5, ((0, 2),)),
        "b_proj": scatter_about(streams_of[9], (D,), 0.3, 2.0),
        "w_up": scatter_about(streams_of[10], (D, FF), D ** -0.5, 0.1875, ((1, 2),)),
        "b_up": scatter_about(streams_of[11], (FF,), 0.5, 3.0, ((0, 2),)),
        "w_down": scatter_about(streams_of[12], (FF, D), FF ** -0.5, 0.09375, ((0, 2),)),
        "b_down": scatter_about(streams_of[13], (D,), 0.3, 2.0),
        "cotangent": scatter_about(streams_of[14], (IMAGES, SEQ, D), 1.0, 6.0, ((0, 32),)),
    }


@jax.custom_vjp
def low(v):
    return lax.optimization_barrier(v.astype(jnp.bfloat16)).astype(jnp.float32)

@jax.custom_vjp
def low_back(v):
    return v

def low_keep(v):
    return (low(v), None)

def low_pass(kept, grad):
    return (grad,)

def back_keep(v):
    return (v, None)

def back_low(kept, grad):
    return (low(grad),)
low.defvjp(low_keep, low_pass)
low_back.defvjp(back_keep, back_low)
NORM_EPS = 1e-06
GELU_C = 0.7978845608028654
GELU_A = 0.044715
HIGHEST_PREC = lax.Precision.HIGHEST

def matmul(left_mat, right_mat):
    return jnp.dot(left_mat, right_mat, precision=HIGHEST_PREC, preferred_element_type=jnp.float32)

def norm_rows(values):
    centre = values - lax.optimization_barrier(jnp.mean(values, axis=-1, keepdims=True))
    return centre * lax.rsqrt(lax.optimization_barrier(jnp.mean(centre * centre, axis=-1, keepdims=True)) + NORM_EPS)

def gelu_tanh(values):
    return 0.5 * values * (1.0 + jnp.tanh(GELU_C * (values + GELU_A * values * values * values)))

def reference(tokens, condition, keep_count, token_order, w_ada, b_ada, w_qkv, b_qv, w_proj, b_proj, w_up, b_up, w_down, b_down, cotangent):
    positions = jnp.arange(SEQ, dtype=jnp.int32)
    in_front = positions[None, :] < keep_count[:, None]
    kept_mask = jnp.any((token_order[:, :, None] == positions[None, None, :]) & in_front[:, :, None], axis=1)
    attn_scale = HD ** (-0.5)
    group_size = 16
    count_groups = IMAGES // group_size

    def forward(x_in, cond_in, params):
        w_ada_f, b_ada_f, w_qkv_f, b_qv_f, w_proj_f, b_proj_f, w_up_f, b_up_f, w_down_f, b_down_f = params
        silu_cond = low(jax.nn.silu(cond_in))
        modulation = low_back(matmul(silu_cond, w_ada_f) + b_ada_f)

        def group_block(pieces):
            x_group, mod_group, kept_group = pieces
            mod_blocks = [mod_group[:, column_block * D:(column_block + 1) * D][:, None, :] for column_block in range(6)]
            shift_one, scale_one, gate_one, shift_two, scale_two, gate_two = mod_blocks
            in_one = low(norm_rows(x_group) * (1.0 + scale_one) + shift_one)
            qkv_rows = matmul(in_one.reshape(-1, D), w_qkv_f.reshape(D, 3 * D)).reshape(group_size, SEQ, 3, HEADS, HD)
            queries = low_back(low(qkv_rows[:, :, 0] + b_qv_f[0].reshape(HEADS, HD)))
            key_rows = low_back(low(qkv_rows[:, :, 1]))
            value_rows = low_back(low(qkv_rows[:, :, 2] + b_qv_f[1].reshape(HEADS, HD)))
            scores = low_back(jnp.einsum('gqhe,gkhe->ghqk', queries, key_rows, precision=HIGHEST_PREC) * attn_scale)
            scores = jnp.where(kept_group[:, None, None, :], scores, -1e+30)
            row_top = lax.optimization_barrier(jnp.max(scores, axis=-1, keepdims=True))
            exp_scores = jnp.exp(scores - row_top)
            prob_rows = low(exp_scores / lax.optimization_barrier(jnp.sum(exp_scores, axis=-1, keepdims=True)))
            attended = low_back(low(jnp.einsum('ghqk,gkhe->gqhe', prob_rows, value_rows, precision=HIGHEST_PREC)))
            branch_one = low_back(matmul(attended.reshape(-1, D), w_proj_f) + b_proj_f).reshape(group_size, SEQ, D)
            resid_one = x_group + gate_one * branch_one
            in_two = low(norm_rows(resid_one) * (1.0 + scale_two) + shift_two)
            pre_act = low_back(matmul(in_two.reshape(-1, D), w_up_f) + b_up_f)
            hidden = low(gelu_tanh(pre_act))
            branch_two = low_back(matmul(hidden, w_down_f) + b_down_f).reshape(group_size, SEQ, D)
            resid_two = resid_one + gate_two * branch_two
            return jnp.where(kept_group[:, :, None], resid_two, x_group)
        group_outs = lax.map(jax.checkpoint(group_block), (x_in.reshape(count_groups, group_size, SEQ, D), modulation.reshape(count_groups, group_size, 6 * D), kept_mask.reshape(count_groups, group_size, SEQ)))
        return group_outs.reshape(IMAGES, SEQ, D)
    params = tuple((weight.astype(jnp.float32) for weight in (w_ada, b_ada, w_qkv, b_qv, w_proj, b_proj, w_up, b_up, w_down, b_down)))
    block_out, pullback = jax.vjp(forward, tokens.astype(jnp.float32), condition.astype(jnp.float32), params)
    grad_tokens, grad_condition, grad_params = pullback(cotangent.astype(jnp.float32))
    return (block_out.astype(jnp.bfloat16), grad_tokens, grad_condition, grad_params[0], grad_params[1], grad_params[2], grad_params[3], grad_params[4], grad_params[5], grad_params[6], grad_params[7], grad_params[8], grad_params[9])
```

```python
import functools

import jax
import jax.numpy as jnp
from jax import lax
from jax.experimental import pallas as pl
from jax.experimental.pallas import tpu as pltpu
from jax.sharding import PartitionSpec as P

HD = 72
LANES = 128
NORM_EPS = 1e-06
MASKED = -1e30
GELU_C = 0.7978845608028654
GELU_A = 0.044715
F32 = jnp.float32
BF16 = jnp.bfloat16


def gelu_tanh(values):
    return 0.5 * values * (1.0 + jnp.tanh(GELU_C * (values + GELU_A * values * values * values)))


def gelu_slope(values):
    tanh_part = jnp.tanh(GELU_C * (values + GELU_A * values * values * values))
    return 0.5 * (1.0 + tanh_part) + 0.5 * values * (1.0 - tanh_part * tanh_part) * GELU_C * (
        1.0 + 3.0 * GELU_A * values * values
    )


def norm_rows(values):
    centre = values - jnp.mean(values, axis=-1, keepdims=True)
    inv_std = lax.rsqrt(jnp.mean(centre * centre, axis=-1, keepdims=True) + NORM_EPS)
    return (centre * inv_std, inv_std)


def norm_back(grad_norm, normed, inv_std):
    return inv_std * (
        grad_norm
        - jnp.mean(grad_norm, axis=-1, keepdims=True)
        - normed * jnp.mean(grad_norm * normed, axis=-1, keepdims=True)
    )


def matmul_nn(left_mat, right_mat):
    return jnp.dot(left_mat, right_mat, preferred_element_type=F32)


def matmul_tn(left_mat, right_mat):
    return lax.dot_general(left_mat, right_mat, (((0,), (0,)), ((), ())), preferred_element_type=F32)


def matmul_nt(left_mat, right_mat):
    return lax.dot_general(left_mat, right_mat, (((1,), (1,)), ((), ())), preferred_element_type=F32)


def head_window(head):
    first = head * HD // LANES * LANES
    last = -(-(head + 1) * HD // LANES) * LANES
    return first, last


def head_mask(head):
    first, last = head_window(head)
    cols = lax.broadcasted_iota(jnp.int32, (1, last - first), 1) + first
    return (cols >= head * HD) & (cols < (head + 1) * HD)


def pick(block_ref, base, head, mask=None):
    first, last = head_window(head)
    block = block_ref[:, base + first : base + last]
    if mask is None:
        return block
    return jnp.where(mask, block, jnp.zeros_like(block))


def add_tiles(tiles, head, block):
    first, last = head_window(head)
    for at in range(first, last, LANES):
        piece = block[:, at - first : at - first + LANES]
        tiles[at] = tiles[at] + piece if at in tiles else piece


def attend_kernel(heads, width, scale, counts_ref, qkv_ref, out_ref):
    rows = qkv_ref.shape[0]
    live = lax.broadcasted_iota(jnp.int32, (1, rows), 1) < counts_ref[pl.program_id(0)]
    tiles = {}
    for head in range(heads):
        mask = head_mask(head)
        scores = matmul_nt(pick(qkv_ref, 0, head, mask), pick(qkv_ref, width, head)) * scale
        scores = jnp.where(live, scores, MASKED)
        exp_scores = jnp.exp(scores - jnp.max(scores, axis=-1, keepdims=True))
        probs = exp_scores / jnp.sum(exp_scores, axis=-1, keepdims=True)
        add_tiles(tiles, head, matmul_nn(probs.astype(BF16), pick(qkv_ref, 2 * width, head, mask)))
    for at, tile in tiles.items():
        out_ref[:, at : at + LANES] = tile.astype(BF16)


def attend_back_kernel(heads, width, scale, counts_ref, qkv_ref, datt_ref, out_ref):
    rows = qkv_ref.shape[0]
    live = lax.broadcasted_iota(jnp.int32, (rows, 1), 0) < counts_ref[pl.program_id(0)]
    tiles = ({}, {}, {})
    for head in range(heads):
        mask = head_mask(head)
        queries = pick(qkv_ref, 0, head, mask)
        key_rows = pick(qkv_ref, width, head, mask)
        grad_att = pick(datt_ref, 0, head, mask)
        scores = jnp.where(live, matmul_nt(key_rows, queries) * scale, MASKED)
        exp_scores = jnp.exp(scores - jnp.max(scores, axis=0, keepdims=True))
        probs = exp_scores / jnp.sum(exp_scores, axis=0, keepdims=True)
        grad_probs = matmul_nt(pick(qkv_ref, 2 * width, head), grad_att)
        inner = jnp.sum(probs * grad_probs, axis=0, keepdims=True)
        grad_scores = (probs * (grad_probs - inner)).astype(BF16)
        add_tiles(tiles[0], head, matmul_tn(grad_scores, key_rows) * scale)
        add_tiles(tiles[1], head, matmul_nn(grad_scores, queries) * scale)
        add_tiles(tiles[2], head, matmul_nn(probs.astype(BF16), grad_att))
    for part in range(3):
        for at, tile in tiles[part].items():
            out_ref[:, part * width + at : part * width + at + LANES] = tile.astype(BF16)


def attend_cost(images, rows, heads, products):
    return pl.CostEstimate(
        flops=2 * products * images * heads * rows * rows * 256,
        bytes_accessed=images * rows * heads * HD * 2 * 8,
        transcendentals=images * heads * rows * rows,
    )


def attend(qkv, counts, rows, heads, width, scale):
    images = counts.shape[0]
    return pl.pallas_call(
        functools.partial(attend_kernel, heads, width, scale),
        grid_spec=pltpu.PrefetchScalarGridSpec(
            num_scalar_prefetch=1,
            grid=(images,),
            in_specs=[pl.BlockSpec((rows, 3 * width), lambda i, c: (i, 0))],
            out_specs=pl.BlockSpec((rows, width), lambda i, c: (i, 0)),
        ),
        out_shape=jax.ShapeDtypeStruct((images * rows, width), BF16),
        cost_estimate=attend_cost(images, rows, heads, 2),
        name="attend",
    )(counts, qkv)


def attend_back(qkv, grad_att, counts, rows, heads, width, scale):
    images = counts.shape[0]
    return pl.pallas_call(
        functools.partial(attend_back_kernel, heads, width, scale),
        grid_spec=pltpu.PrefetchScalarGridSpec(
            num_scalar_prefetch=1,
            grid=(images,),
            in_specs=[
                pl.BlockSpec((rows, 3 * width), lambda i, c: (i, 0)),
                pl.BlockSpec((rows, width), lambda i, c: (i, 0)),
            ],
            out_specs=pl.BlockSpec((rows, 3 * width), lambda i, c: (i, 0)),
        ),
        out_shape=jax.ShapeDtypeStruct((images * rows, 3 * width), BF16),
        cost_estimate=attend_cost(images, rows, heads, 5),
        name="attend_back",
    )(counts, qkv, grad_att)


def from_peer(value, size):
    return lax.ppermute(value, "tensor", [((i + 1) % size, i) for i in range(size)])


def gather_chunks(value, size):
    if size == 1:
        return [value]
    if size == 2:
        return [value, from_peer(value, size)]
    whole = lax.all_gather(value, "tensor", axis=0)
    whole = jnp.roll(whole, -lax.axis_index("tensor"), axis=0)
    return [whole[k] for k in range(size)]


def whole_sums(parts, size):
    if size == 1:
        return [parts[0].astype(F32)]
    if size == 2:
        return [
            parts[0].astype(F32) + from_peer(parts[1], size).astype(F32),
            parts[1].astype(F32) + from_peer(parts[0], size).astype(F32),
        ]
    me = lax.axis_index("tensor")
    whole = lax.psum(jnp.roll(jnp.stack(parts), me, axis=0), "tensor")
    whole = jnp.roll(whole, -me, axis=0).astype(F32)
    return [whole[k] for k in range(size)]


def own_sum(parts, size):
    if size == 1:
        return parts[0]
    if size == 2:
        return parts[0] + from_peer(parts[1].astype(BF16), size).astype(F32)
    me = lax.axis_index("tensor")
    whole = jnp.roll(jnp.stack(parts).astype(BF16), me, axis=0)
    return lax.psum_scatter(whole, "tensor", scatter_dimension=0, tiled=False).astype(F32)


def closed_path(chips):
    deep = 4 if chips % 4 == 0 else 1
    wide = chips // deep
    path = [(0, 0)] if wide > 1 else []
    for row in range(deep):
        line = range(min(1, wide - 1), wide)
        path += [(row, col) for col in (line if row % 2 == 0 else reversed(line))]
    if wide > 1:
        path += [(row, 0) for row in range(deep - 1, 0, -1)]
    return [row * wide + col for row, col in path]


class Ring:
    def __init__(self, groups, flip=False):
        self.groups, self.chips = groups, groups // 2
        self.usable = groups % 2 == 0 and self.chips >= 3
        if not self.usable:
            return
        self.path = closed_path(self.chips)
        if flip:
            self.path = self.path[::-1]
        self.far = self.chips // 2
        self.near = self.chips - 1 - self.far
        me = lax.axis_index("dp")
        self.core = me % 2
        place = [self.path.index(chip) for chip in range(self.chips)]
        self.spot = jnp.asarray(place, jnp.int32)[me // 2]

    def hop(self, value, step):
        path = self.path
        pairs = [
            (2 * path[n] + c, 2 * path[(n + step) % self.chips] + c)
            for n in range(self.chips)
            for c in (0, 1)
        ]
        return lax.ppermute(value, "dp", pairs)

    def partner(self, value):
        return lax.ppermute(value, "dp", [(n, n ^ 1) for n in range(self.groups)])

    def at(self, ahead):
        return lax.rem(self.spot + ahead + self.chips, self.chips)

    def spread(self, value):
        found = [(0, value)]
        front = back = value
        for ahead in range(1, self.far + 1):
            if ahead <= self.near:
                front = self.hop(front, 1)
                found.append((-ahead, front))
            back = self.hop(back, -1)
            found.append((ahead, back))
        return found

    def gather(self, value):
        if not self.usable:
            return lax.all_gather(value, "dp", axis=0)
        column = jnp.stack([piece for _, piece in self.spread(value)])
        return jnp.concatenate([column, self.partner(column)])

    def sum(self, mat):
        height, breadth = mat.shape
        if not self.usable or height % (8 * self.groups):
            return lax.psum(mat, "dp")

        def added(*terms):
            return sum(term.astype(F32) for term in terms).astype(BF16)

        halves = mat.reshape(2, self.chips, height // self.groups, breadth)
        half = lambda which: lax.dynamic_index_in_dim(halves, which, 0, keepdims=False)
        held = added(half(self.core), self.partner(half(1 - self.core)))
        block = lambda ahead: lax.dynamic_index_in_dim(held, self.at(ahead), 0, keepdims=False)
        front, back = block(self.far), block(-self.near)
        for left in range(self.far - 1, 0, -1):
            front = added(self.hop(front, 1), block(left))
            if left < self.near:
                back = added(self.hop(back, -1), block(-left))
        whole = added(block(0), self.hop(front, 1), self.hop(back, -1))
        summed = jnp.zeros_like(held)
        for ahead, value in self.spread(whole):
            summed = lax.dynamic_update_index_in_dim(summed, value, self.at(ahead), 0)
        other = self.partner(summed)
        first = jnp.where(self.core == 0, summed, other)
        second = jnp.where(self.core == 0, other, summed)
        return jnp.concatenate([first, second]).reshape(height, breadth)


def body(
    size,
    groups,
    tokens,
    condition,
    keep_count,
    token_order,
    w_ada,
    b_ada,
    w_qkv,
    b_qv,
    w_proj,
    b_proj,
    w_up,
    b_up,
    w_down,
    b_down,
    cotangent,
):
    own, seq, feat = tokens.shape
    kept = 3 * seq // 4
    rows = own * kept
    cols = w_qkv.shape[2]
    heads = cols // HD
    width = -(-cols // LANES) * LANES
    scale = HD ** (-0.5)
    me = lax.axis_index("tensor")
    chunks = range(size)
    ring, back_ring = Ring(groups), Ring(groups, flip=True)

    counts = jnp.roll(keep_count, -me * own)
    own_counts = counts[:own]
    chunk_counts = [counts[k * own : (k + 1) * own] for k in chunks]

    slots = jnp.arange(kept, dtype=jnp.int32)
    places = jnp.arange(seq, dtype=jnp.int32)
    chosen = (token_order[:, :kept, None] == places) & (
        slots[None, :, None] < own_counts[:, None, None]
    )
    select = chosen.astype(BF16)
    kept_pos = jnp.any(chosen, axis=1)

    def picked(values):
        return jnp.einsum("isp,ipd->isd", select, values, preferred_element_type=F32).astype(BF16)

    x_chunks = gather_chunks(picked(tokens), size)
    cot_chunks = gather_chunks(picked(cotangent), size)

    cond = jnp.roll(condition, -me * own, axis=0).astype(F32)
    silu_cond = jax.nn.silu(cond).astype(BF16)
    mod_part = matmul_nn(silu_cond, w_ada)
    mod_sum = whole_sums([mod_part[k * own : (k + 1) * own] for k in chunks], size)
    mods = [
        [block[:, None, :] for block in jnp.split(mod_sum[k] + b_ada.astype(F32), 6, axis=1)]
        for k in chunks
    ]

    qkv_weight = jnp.pad(w_qkv, ((0, 0), (0, 0), (0, width - cols))).reshape(feat, 3 * width)
    proj_weight = jnp.pad(w_proj, ((0, width - cols), (0, 0)))
    bias_q, bias_v = b_qv.astype(F32)
    zero_pad = jnp.zeros((width - cols,), F32)
    qkv_bias = jnp.concatenate(
        [bias_q, zero_pad, jnp.zeros((width,), F32), bias_v, zero_pad]
    )

    def flat(values):
        return values.reshape(rows, feat)

    def images(values):
        return values.reshape(own, kept, feat)

    in_one, qkv, att, proj_part, normed_one, inv_one = ([None] * size for _ in range(6))
    for k in chunks:
        shift_one, scale_one = mods[k][0], mods[k][1]
        normed_one[k], inv_one[k] = norm_rows(x_chunks[k].astype(F32))
        in_one[k] = flat((normed_one[k] * (1.0 + scale_one) + shift_one).astype(BF16))
        qkv[k] = (matmul_nn(in_one[k], qkv_weight) + qkv_bias).astype(BF16)
        att[k] = attend(qkv[k], chunk_counts[k], kept, heads, width, scale)
        proj_part[k] = matmul_nn(att[k], proj_weight).astype(BF16)
    proj_sum = whole_sums(proj_part, size)

    branch_one, normed_two, inv_two, in_two, grad_two, hidden, resid = (
        [None] * size for _ in range(7)
    )
    grad_branch_two, grad_pre, down_part, up_part = ([None] * size for _ in range(4))
    for k in reversed(chunks):
        gate_one, shift_two, scale_two, gate_two = mods[k][2:]
        branch_one[k] = images(proj_sum[k] + b_proj.astype(F32))
        resid[k] = x_chunks[k].astype(F32) + gate_one * branch_one[k]
        normed_two[k], inv_two[k] = norm_rows(resid[k])
        in_two[k] = flat((normed_two[k] * (1.0 + scale_two) + shift_two).astype(BF16))
        pre_act = matmul_nn(in_two[k], w_up) + b_up.astype(F32)
        grad_two[k] = cot_chunks[k].astype(F32)
        grad_branch_two[k] = flat((gate_two * grad_two[k]).astype(BF16))
        grad_pre[k] = (matmul_nt(grad_branch_two[k], w_down) * gelu_slope(pre_act)).astype(BF16)
        up_part[k] = matmul_nt(grad_pre[k], w_up).astype(BF16)
        hidden[k] = gelu_tanh(pre_act).astype(BF16)
        down_part[k] = matmul_nn(hidden[k], w_down)
    grad_in_two = whole_sums(up_part, size)

    hidden_all = jnp.concatenate(hidden)
    grad_branch_two_all = jnp.concatenate(grad_branch_two)
    grad_pre_all = jnp.concatenate(grad_pre)
    grad_w_down = matmul_tn(hidden_all, grad_branch_two_all).astype(BF16)
    grad_w_up = matmul_tn(jnp.concatenate(in_two), grad_pre_all).astype(BF16)
    (grad_two, grad_w_down, grad_w_up) = lax.optimization_barrier(
        (grad_two, grad_w_down, grad_w_up)
    )
    grad_w_down, grad_w_up = ring.sum(grad_w_down), back_ring.sum(grad_w_up)
    grad_b_down = jnp.sum(grad_branch_two_all, axis=0, dtype=F32)
    grad_b_up = jnp.sum(grad_pre_all, axis=0, dtype=F32)

    branch_two = images(own_sum(down_part, size) + b_down.astype(F32))
    resid_two = (resid[0] + mods[0][5] * branch_two).astype(BF16)
    placed_out = jnp.einsum("isp,isd->ipd", select, resid_two, preferred_element_type=F32)
    block_out = jnp.where(kept_pos[:, :, None], placed_out.astype(BF16), tokens)
    grad_gate_two = jnp.sum(grad_two[0] * branch_two, axis=1)

    grad_one, grad_branch_one, grad_qkv, one_part = ([None] * size for _ in range(4))
    for k in chunks:
        gate_one, scale_two = mods[k][2], mods[k][4]
        grad_in = images(grad_in_two[k])
        grad_one[k] = grad_two[k] + norm_back(
            grad_in * (1.0 + scale_two), normed_two[k], inv_two[k]
        )
        grad_branch_one[k] = flat((gate_one * grad_one[k]).astype(BF16))
        grad_att = matmul_nt(grad_branch_one[k], proj_weight).astype(BF16)
        grad_qkv[k] = attend_back(
            qkv[k], grad_att, chunk_counts[k], kept, heads, width, scale
        )
        one_part[k] = matmul_nt(grad_qkv[k], qkv_weight)
    grad_in_one = images(own_sum(one_part, size))

    grad_branch_one_all = jnp.concatenate(grad_branch_one)
    grad_qkv_all = jnp.concatenate(grad_qkv)
    grad_w_proj = matmul_tn(grad_branch_one_all, jnp.concatenate(att)).astype(BF16)
    grad_w_qkv = matmul_tn(jnp.concatenate(in_one), grad_qkv_all).astype(BF16)
    grad_w_att = ring.sum(jnp.concatenate([grad_w_qkv, grad_w_proj], axis=1))
    grad_w_att = grad_w_att.astype(F32).reshape(feat, 4, width)[:, :, :cols]
    grad_b_proj = jnp.sum(grad_branch_one_all, axis=0, dtype=F32)
    grad_b_qkv = jnp.sum(grad_qkv_all, axis=0, dtype=F32)

    grad_mid = images(grad_in_two[0])
    grad_shift_two = jnp.sum(grad_mid, axis=1)
    grad_scale_two = jnp.sum(grad_mid * normed_two[0], axis=1)
    grad_gate_one = jnp.sum(grad_one[0] * branch_one[0], axis=1)
    grad_shift_one = jnp.sum(grad_in_one, axis=1)
    grad_scale_one = jnp.sum(grad_in_one * normed_one[0], axis=1)
    grad_rows = grad_one[0] + norm_back(
        grad_in_one * (1.0 + mods[0][1]), normed_one[0], inv_one[0]
    )
    high = lax.reduce_precision(grad_rows, 8, 7)
    placed_grad = jnp.einsum(
        "isp,isd->ipd", select, high.astype(BF16), preferred_element_type=F32
    ) + jnp.einsum(
        "isp,isd->ipd", select, (grad_rows - high).astype(BF16), preferred_element_type=F32
    )
    grad_tokens = jnp.where(kept_pos[:, :, None], placed_grad, cotangent.astype(F32))

    grad_mod = jnp.concatenate(
        [
            grad_shift_one,
            grad_scale_one,
            grad_gate_one,
            grad_shift_two,
            grad_scale_two,
            grad_gate_two,
        ],
        axis=1,
    ).astype(BF16)
    grad_mod = jnp.concatenate(gather_chunks(grad_mod, size))
    sigmoid_c = jax.nn.sigmoid(cond)
    grad_condition = matmul_nt(grad_mod, w_ada) * (sigmoid_c * (1.0 + cond * (1.0 - sigmoid_c)))
    grad_condition = jnp.roll(grad_condition, me * own, axis=0)

    biases = jnp.concatenate(
        [grad_b_qkv[:cols], grad_b_qkv[2 * width : 2 * width + cols], grad_b_proj, grad_b_up, grad_b_down]
    ).astype(BF16)
    pieces = [grad_mod.reshape(-1), silu_cond.reshape(-1), biases]
    packed = ring.gather(jnp.concatenate(pieces))
    first, second = pieces[0].size, pieces[0].size + pieces[1].size
    grad_mod_all = packed[:, :first].reshape(-1, 6 * feat)
    silu_all = packed[:, first:second].reshape(-1, silu_cond.shape[1])
    bias_sums = jnp.sum(packed[:, second:], axis=0, dtype=F32)
    grad_w_ada = matmul_tn(silu_all, grad_mod_all)
    grad_b_ada = jnp.sum(grad_mod_all, axis=0, dtype=F32)
    hid = w_up.shape[1]
    cuts = [0, 2 * cols, 2 * cols + feat, 2 * cols + feat + hid, 2 * cols + 2 * feat + hid]
    grad_b_qv, grad_b_proj, grad_b_up, grad_b_down = (
        bias_sums[cuts[n] : cuts[n + 1]] for n in range(4)
    )
    return (
        block_out,
        grad_tokens,
        grad_condition,
        grad_w_ada,
        grad_b_ada,
        grad_w_att[:, :3],
        grad_b_qv.reshape(2, cols),
        grad_w_att[:, 3].T,
        grad_b_proj,
        grad_w_up.astype(F32),
        grad_b_up,
        grad_w_down.astype(F32),
        grad_b_down,
    )


def solution(mesh):
    placed = (
        P(("dp", "tensor"), None, None),
        P("dp", "tensor"),
        P("dp"),
        P(("dp", "tensor"), None),
        P("tensor", None),
        P(),
        P(None, None, "tensor"),
        P(None, "tensor"),
        P("tensor", None),
        P(),
        P(None, "tensor"),
        P("tensor"),
        P("tensor", None),
        P(),
        P(("dp", "tensor"), None, None),
    )
    return jax.shard_map(
        functools.partial(body, mesh.shape["tensor"], mesh.shape["dp"]),
        mesh=mesh,
        in_specs=placed,
        out_specs=(
            P(("dp", "tensor"), None, None),
            P(("dp", "tensor"), None, None),
            P("dp", "tensor"),
            P("tensor", None),
            P(),
            P(None, None, "tensor"),
            P(None, "tensor"),
            P("tensor", None),
            P(),
            P(None, "tensor"),
            P("tensor"),
            P("tensor", None),
            P(),
        ),
        check_vma=False,
    )
```
